32 devices in a mesh: row: 4 (over x, core), col: 2 (over y), depth: 4 (over z).
Axes of the slice: x: 2, y: 2, z: 4, core: 2. Of those that a mesh axis runs over, the one named last changes fastest.
Arguments:
- tokens: bfloat16 [64, 6144], P(('col', 'depth'), 'row'), may hold values from -6 to 6
- first_weight: bfloat16 [6144, 24576], P('row', ('col', 'depth')), may hold values from -0.078125 to 0.078125
- first_tangent: bfloat16 [6144, 24576], P('row', ('col', 'depth')), may hold values from -0.078125 to 0.078125
- second_weight: bfloat16 [24576, 6144], P(('col', 'depth'), 'row'), may hold values from -0.0390625 to 0.0390625
- second_tangent: bfloat16 [24576, 6144], P(('col', 'depth'), 'row'), may hold values from -0.0390625 to 0.0390625
Outputs:
- grad_first: float32 [6144, 24576], P('row', ('col', 'depth'))
- grad_second: float32 [24576, 6144], P(('col', 'depth'), 'row')
The draws below stay inside these ranges and needn't reach their ends.
All inputs are finite; a program needn't handle non-finite values.
Results may differ from the reference program's by a relative error of at most 0.0047.
Values may be sent and summed in bfloat16 or wider, within the bound.
A program may use at most 192 MiB of HBM per device.

```python
import math
import jax
import jax.numpy as jnp
from jax import lax

D = 6144
FF = 24576
TOKENS = 64


def shard_levels(stream_key, extent, split, smallest, high):
    gain = 1.0
    for axis_at, blocks in split:
        steps = jax.random.uniform(jax.random.fold_in(jax.random.fold_in(stream_key, 6), axis_at), (blocks,), jnp.float32, smallest / len(split), high / len(split))
        gain = gain * jnp.repeat(jnp.exp(steps), extent[axis_at] // blocks).reshape((-1,) + (1,) * (len(extent) - 1 - axis_at))
    return gain


def centred(stream_key, shape, width, bound, split=(), held_as=jnp.bfloat16):
    array = width * jax.random.normal(stream_key, shape, jnp.float32)
    if split:
        array = array * shard_levels(stream_key, shape, split, -0.22, 0.18)
    return jnp.clip(array, -bound, bound).astype(held_as)


def setup_inputs(seed: int = 0) -> dict:
    seeds = jax.random.split(jax.random.key(seed), 6)
    return {
        "tokens": centred(seeds[0], (TOKENS, D), 1.0, 6.0, ((0, 8), (1, 4))),
        "first_weight": centred(seeds[1], (D, FF), D ** -0.5, 0.078125, ((0, 4), (1, 8))),
        "first_tangent": centred(seeds[2], (D, FF), D ** -0.5, 0.078125, ((0, 4), (1, 8))),
        "second_weight": centred(seeds[3], (FF, D), FF ** -0.5, 0.0390625, ((0, 8), (1, 4))),
        "second_tangent": centred(seeds[4], (FF, D), FF ** -0.5, 0.0390625, ((0, 8), (1, 4))),
    }


def reference(tokens, first_weight, first_tangent, second_weight, second_tangent):
    hidden = jnp.dot(tokens, first_weight, preferred_element_type=jnp.float32)
    hidden_tan = jnp.dot(tokens, first_tangent, preferred_element_type=jnp.float32)
    inner = 0.7978845608 * (hidden + 0.044715 * hidden * hidden * hidden)
    tval = jnp.tanh(inner)
    active = (0.5 * hidden * (1.0 + tval)).astype(jnp.bfloat16)
    slopes = 0.5 * (1.0 + tval) + 0.5 * hidden * (1.0 - tval * tval) * 0.7978845608 * (1.0 + 3.0 * 0.044715 * hidden * hidden)
    active_tan = (slopes * hidden_tan).astype(jnp.bfloat16)
    out_tan = (jnp.dot(active_tan, second_weight, preferred_element_type=jnp.float32) + jnp.dot(active, second_tangent, preferred_element_type=jnp.float32)).astype(jnp.bfloat16)
    backward = lax.dot_general(out_tan, second_weight, (((1,), (1,)), ((), ())), preferred_element_type=jnp.float32)
    back_hidden = (backward * slopes).astype(jnp.bfloat16)
    factor = 1.0 / math.sqrt(TOKENS)
    grad_second = lax.dot_general(active, out_tan, (((0,), (0,)), ((), ())), preferred_element_type=jnp.float32) * factor
    grad_first = lax.dot_general(tokens, back_hidden, (((0,), (0,)), ((), ())), preferred_element_type=jnp.float32) * factor
    return (grad_first, grad_second)
```

```python
import functools
import math

import jax
import jax.numpy as jnp
from jax import lax
from jax.experimental import pallas as pl
from jax.experimental.pallas import tpu as pltpu
from jax.sharding import PartitionSpec as P

CORES = 2
LANES = 128
F32 = jnp.float32
BF16 = jnp.bfloat16


def pieces(extent, most):
    return max(n for n in range(1, most + 1) if extent % (n * LANES) == 0)


def gelu_parts(hidden, hidden_tan):
    inner = 0.7978845608 * (hidden + 0.044715 * hidden * hidden * hidden)
    tval = jnp.tanh(inner)
    active = 0.5 * hidden * (1.0 + tval)
    slopes = 0.5 * (1.0 + tval) + 0.5 * hidden * (1.0 - tval * tval) * 0.7978845608 * (
        1.0 + 3.0 * 0.044715 * hidden * hidden
    )
    return active, slopes * hidden_tan, slopes


def block_kernel(
    sizes,
    tok_ref, fw_ref, ft_ref, sw_ref, st_ref,
    tok_out, act_out, tan_out, back_out,
    w1, w2, tokg, tok2d, hbuf, psend, precv, xsend, xrecv, acts, slopes,
    acc, rsend, rrecv, outg, bsend, brecv, bxsend, bxrecv, back,
    wsem, tok_s, tok_r, ps, pr, xs, xr, as_, ar, rs, rr, gs, gr, bps, bpr, bxs, bxr, bas, bar_,
):
    chips, ncol, ndepth, nf, no = sizes
    group = ncol * ndepth
    tl, dl = tok_ref.shape
    total = group * tl
    half = total // CORES
    cw = w1.shape[-1]
    dn = dl // no

    row = lax.axis_index("row")
    core = lax.rem(row, CORES)
    chip = lax.div(row, CORES)
    mate = {"row": chip * CORES + (1 - core)}
    across = [{"row": lax.rem(chip + o, chips) * CORES + core} for o in range(1, chips)]
    me = lax.axis_index("col") * ndepth + lax.axis_index("depth")
    ranks = [lax.rem(me + o, group) for o in range(1, group)]
    peers = [{"col": lax.div(r, ndepth), "depth": lax.rem(r, ndepth)} for r in ranks]
    mine = pl.ds(pl.multiple_of(core * half, half), half)
    other = pl.ds(pl.multiple_of((1 - core) * half, half), half)

    loads = {}
    for i, ref in enumerate((fw_ref, ft_ref)):
        for k in range(nf):
            loads[i, k] = pltpu.make_async_copy(
                ref.at[:, pl.ds(k * cw, cw)], w1.at[i, k], wsem.at[i, k]
            )
    for i, ref in enumerate((sw_ref, st_ref)):
        for k in range(nf):
            loads[2 + i, k] = pltpu.make_async_copy(
                ref.at[pl.ds(k * cw, cw), :], w2.at[i, k], wsem.at[2 + i, k]
            )
    for pair in (0, 2):
        for k in range(nf):
            loads[pair, k].start()
            loads[pair + 1, k].start()

    sent = []

    def send(src, dst, ssem, rsem, device):
        copy = pltpu.make_async_remote_copy(
            src_ref=src, dst_ref=dst, send_sem=ssem, recv_sem=rsem,
            device_id=device, device_id_type=pl.DeviceIdType.MESH,
        )
        copy.start()
        sent.append(copy)
        return copy

    barrier = pltpu.get_barrier_semaphore()
    everyone = [mate] + across + peers
    for device in everyone:
        pl.semaphore_signal(
            barrier, inc=1, device_id=device, device_id_type=pl.DeviceIdType.MESH
        )
    pl.semaphore_wait(barrier, len(everyone))

    arrivals = [
        send(tok_ref, tokg.at[me], tok_s.at[o], tok_r.at[o], device)
        for o, device in enumerate(peers)
    ]
    tokg[me] = tok_ref[...]
    for copy in arrivals:
        copy.wait_recv()
    tok2d[...] = tokg[...].astype(F32).reshape(total, dl).astype(BF16)
    tok_out[...] = tok2d[...]

    cols = [pl.ds(k * cw, cw) for k in range(nf)]
    to_mate, to_chips, halves = {}, {}, {}

    def first(k):
        for i in range(2):
            loads[i, k].wait()
            hbuf[i, :, cols[k]] = jnp.dot(tok2d[...], w1[i, k], preferred_element_type=F32)
            psend[k, i] = hbuf[i, other, cols[k]]
        to_mate[k] = send(psend.at[k], precv.at[k], ps.at[k], pr.at[k], mate)

    def chip_sum(k):
        to_mate[k].wait_recv()
        for i in range(2):
            both = hbuf[i, mine, cols[k]] + precv[k, i]
            hbuf[i, mine, cols[k]] = both
            xsend[k, i] = both.astype(BF16)
        to_chips[k] = [
            send(xsend.at[k], xrecv.at[o, k], xs.at[o, k], xr.at[o, k], device)
            for o, device in enumerate(across)
        ]

    def activate(k):
        hidden, hidden_tan = hbuf[0, mine, cols[k]], hbuf[1, mine, cols[k]]
        for o, copy in enumerate(to_chips[k]):
            copy.wait_recv()
            hidden = hidden + xrecv[o, k, 0].astype(F32)
            hidden_tan = hidden_tan + xrecv[o, k, 1].astype(F32)
        active, active_tan, slope = gelu_parts(hidden, hidden_tan)
        acts[k, 0, mine, :] = active_tan.astype(BF16)
        acts[k, 1, mine, :] = active.astype(BF16)
        slopes[:, cols[k]] = slope
        part = acts.at[k, :, mine, :]
        halves[k] = send(part, part, as_.at[k], ar.at[k], mate)

    scatter, gather = {}, {}

    def second(k):
        halves[k].wait_recv()
        for i in range(2):
            loads[2 + i, k].wait()
        for n in range(no):
            part = pl.ds(n * dn, dn)
            term = jnp.dot(acts[k, 0], w2[0, k, :, part], preferred_element_type=F32)
            term += jnp.dot(acts[k, 1], w2[1, k, :, part], preferred_element_type=F32)
            if k > 0:
                term += acc[n]
            acc[n] = term
            if k == nf - 1:
                rsend[n] = term.reshape(group, tl, dn).astype(BF16)
                scatter[n] = [
                    send(rsend.at[n, r], rrecv.at[n, o], rs.at[n, o], rr.at[n, o], device)
                    for o, (r, device) in enumerate(zip(ranks, peers))
                ]

    for t in range(nf + 5):
        for lag, stage in ((0, first), (1, chip_sum), (3, activate), (5, second)):
            if 0 <= t - lag < nf:
                stage(t - lag)

    for n in range(no):
        value = acc[n, pl.ds(pl.multiple_of(me * tl, tl), tl), :]
        for o, copy in enumerate(scatter[n]):
            copy.wait_recv()
            value += rrecv[n, o].astype(F32)
        outg[n, me] = value.astype(BF16)
        gather[n] = [
            send(outg.at[n, me], outg.at[n, me], gs.at[n, o], gr.at[n, o], device)
            for o, device in enumerate(peers)
        ]

    to_mate, to_chips, halves = {}, {}, {}

    def back_chip_sum(k):
        to_mate[k].wait_recv()
        both = hbuf[0, mine, cols[k]] + brecv[k]
        hbuf[0, mine, cols[k]] = both
        bxsend[k] = both.astype(BF16)
        to_chips[k] = [
            send(bxsend.at[k], bxrecv.at[o, k], bxs.at[o, k], bxr.at[o, k], device)
            for o, device in enumerate(across)
        ]

    def back_finish(k):
        value = hbuf[0, mine, cols[k]]
        for o, copy in enumerate(to_chips[k]):
            copy.wait_recv()
            value += bxrecv[o, k].astype(F32)
        back[k, mine, :] = (value * slopes[:, cols[k]]).astype(BF16)
        part = back.at[k, mine, :]
        halves[k] = send(part, part, bas.at[k], bar_.at[k], mate)

    for n in range(no):
        for copy in gather[n]:
            copy.wait_recv()
        part = pl.ds(n * dn, dn)
        tan_out[:, part] = outg[n].astype(F32).reshape(total, dn).astype(BF16)
        for k in range(nf):
            term = lax.dot_general(
                tan_out[:, part], w2[0, k, :, part], (((1,), (1,)), ((), ())),
                preferred_element_type=F32,
            )
            if n > 0:
                term += hbuf[0, :, cols[k]]
            hbuf[0, :, cols[k]] = term
            if n == no - 1:
                bsend[k] = hbuf[0, other, cols[k]]
                to_mate[k] = send(bsend.at[k], brecv.at[k], bps.at[k], bpr.at[k], mate)
                if k >= 1:
                    back_chip_sum(k - 1)
                if k >= 3:
                    back_finish(k - 3)
    back_chip_sum(nf - 1)
    for k in range(max(0, nf - 3), nf):
        back_finish(k)
    for k in range(nf):
        act_out[k] = acts[k, 1]
    for k in range(nf):
        halves[k].wait_recv()
        back_out[k] = back[k]
    for copy in sent:
        copy.wait_send()


def grads_kernel(factor, tok_ref, act_ref, tan_ref, back_ref, first_ref, second_ref):
    lhs_rows = (((0,), (0,)), ((), ()))
    second_ref[...] = (
        lax.dot_general(act_ref[0], tan_ref[...], lhs_rows, preferred_element_type=F32) * factor
    )
    first_ref[...] = (
        lax.dot_general(tok_ref[...], back_ref[0], lhs_rows, preferred_element_type=F32) * factor
    )


def on_device(axes, tokens, first_weight, first_tangent, second_weight, second_tangent):
    tl, dl = tokens.shape
    fl = first_weight.shape[1]
    ncol, ndepth, chips = axes["col"], axes["depth"], axes["row"] // CORES
    group = ncol * ndepth
    total, half = group * tl, group * tl // CORES
    nf, no = pieces(fl, 6), pieces(dl, 2)
    cw, dn = fl // nf, dl // no
    far = max(chips - 1, 1)
    dma = pltpu.SemaphoreType.DMA
    whole = pl.BlockSpec(memory_space=pltpu.VMEM)
    hbm = pl.BlockSpec(memory_space=pl.ANY)
    gathered, active, out_tan, back_hidden = pl.pallas_call(
        functools.partial(block_kernel, (chips, ncol, ndepth, nf, no)),
        name="block",
        out_shape=(
            jax.ShapeDtypeStruct((total, dl), BF16),
            jax.ShapeDtypeStruct((nf, total, cw), BF16),
            jax.ShapeDtypeStruct((total, dl), BF16),
            jax.ShapeDtypeStruct((nf, total, cw), BF16),
        ),
        in_specs=[whole, hbm, hbm, hbm, hbm],
        out_specs=(whole,) * 4,
        scratch_shapes=[
            pltpu.VMEM((2, nf, dl, cw), BF16),
            pltpu.VMEM((2, nf, cw, dl), BF16),
            pltpu.VMEM((group, tl, dl), BF16),
            pltpu.VMEM((total, dl), BF16),
            pltpu.VMEM((2, total, fl), F32),
            pltpu.VMEM((nf, 2, half, cw), F32),
            pltpu.VMEM((nf, 2, half, cw), F32),
            pltpu.VMEM((nf, 2, half, cw), BF16),
            pltpu.VMEM((far, nf, 2, half, cw), BF16),
            pltpu.VMEM((nf, 2, total, cw), BF16),
            pltpu.VMEM((half, fl), F32),
            pltpu.VMEM((no, total, dn), F32),
            pltpu.VMEM((no, group, tl, dn), BF16),
            pltpu.VMEM((no, group - 1, tl, dn), BF16),
            pltpu.VMEM((no, group, tl, dn), BF16),
            pltpu.VMEM((nf, half, cw), F32),
            pltpu.VMEM((nf, half, cw), F32),
            pltpu.VMEM((nf, half, cw), BF16),
            pltpu.VMEM((far, nf, half, cw), BF16),
            pltpu.VMEM((nf, total, cw), BF16),
            dma((4, nf)),
            dma((group - 1,)), dma((group - 1,)),
            dma((nf,)), dma((nf,)),
            dma((far, nf)), dma((far, nf)),
            dma((nf,)), dma((nf,)),
            dma((no, group - 1)), dma((no, group - 1)),
            dma((no, group - 1)), dma((no, group - 1)),
            dma((nf,)), dma((nf,)),
            dma((far, nf)), dma((far, nf)),
            dma((nf,)), dma((nf,)),
        ],
        compiler_params=pltpu.CompilerParams(
            collective_id=0, has_side_effects=True, vmem_limit_bytes=62 * 1024 * 1024
        ),
    )(tokens, first_weight, first_tangent, second_weight, second_tangent)

    return pl.pallas_call(
        functools.partial(grads_kernel, 1.0 / math.sqrt(total)),
        name="grads",
        grid=(nf,),
        out_shape=(
            jax.ShapeDtypeStruct((dl, fl), F32),
            jax.ShapeDtypeStruct((fl, dl), F32),
        ),
        in_specs=[
            pl.BlockSpec((total, dl), lambda k: (0, 0)),
            pl.BlockSpec((1, total, cw), lambda k: (k, 0, 0)),
            pl.BlockSpec((total, dl), lambda k: (0, 0)),
            pl.BlockSpec((1, total, cw), lambda k: (k, 0, 0)),
        ],
        out_specs=(
            pl.BlockSpec((dl, cw), lambda k: (0, k)),
            pl.BlockSpec((cw, dl), lambda k: (k, 0)),
        ),
    )(gathered, active, out_tan, back_hidden)


def solution(mesh):
    return jax.shard_map(
        functools.partial(on_device, dict(mesh.shape)),
        mesh=mesh,
        in_specs=(
            P(("col", "depth"), "row"),
            P("row", ("col", "depth")),
            P("row", ("col", "depth")),
            P(("col", "depth"), "row"),
            P(("col", "depth"), "row"),
        ),
        out_specs=(P("row", ("col", "depth")), P(("col", "depth"), "row")),
        check_vma=False,
    )
```

```python
import functools
import math

import jax
import jax.numpy as jnp
from jax import lax
from jax.experimental import pallas as pl
from jax.experimental.pallas import tpu as pltpu
from jax.sharding import PartitionSpec as P

CORES = 2
LANES = 128
F32 = jnp.float32
BF16 = jnp.bfloat16


def pieces(extent, most):
    return max(n for n in range(1, most + 1) if extent % (n * LANES) == 0)


def gelu_parts(hidden, hidden_tan):
    inner = 0.7978845608 * (hidden + 0.044715 * hidden * hidden * hidden)
    tval = jnp.tanh(inner)
    active = 0.5 * hidden * (1.0 + tval)
    slopes = 0.5 * (1.0 + tval) + 0.5 * hidden * (1.0 - tval * tval) * 0.7978845608 * (
        1.0 + 3.0 * 0.044715 * hidden * hidden
    )
    return active, slopes * hidden_tan, slopes


def block_kernel(
    sizes,
    tok_ref, fw_ref, ft_ref, sw_ref, st_ref,
    tok_out, act_out, tan_out, back_out,
    w1, w2, tokg, tok2d, hbuf, psend, precv, xsend, xrecv, acts, slopes,
    acc, rsend, rrecv, outg, bsend, brecv, bxsend, bxrecv, back,
    wsem, tok_s, tok_r, ps, pr, xs, xr, as_, ar, rs, rr, gs, gr, bps, bpr, bxs, bxr, bas, bar_,
):
    chips, ncol, ndepth, nf, no = sizes
    group = ncol * ndepth
    tl, dl = tok_ref.shape
    total = group * tl
    half = total // CORES
    cw = w1.shape[-1]
    dn = dl // no

    row = lax.axis_index("row")
    core = lax.rem(row, CORES)
    chip = lax.div(row, CORES)
    mate = {"row": chip * CORES + (1 - core)}
    across = [{"row": lax.rem(chip + o, chips) * CORES + core} for o in range(1, chips)]
    me = lax.axis_index("col") * ndepth + lax.axis_index("depth")
    ranks = [lax.rem(me + o, group) for o in range(1, group)]
    peers = [{"col": lax.div(r, ndepth), "depth": lax.rem(r, ndepth)} for r in ranks]
    mine = pl.ds(pl.multiple_of(core * half, half), half)
    other = pl.ds(pl.multiple_of((1 - core) * half, half), half)

    loads = {}
    for i, ref in enumerate((fw_ref, ft_ref)):
        for k in range(nf):
            loads[i, k] = pltpu.make_async_copy(
                ref.at[:, pl.ds(k * cw, cw)], w1.at[i, k], wsem.at[i, k]
            )
    for i, ref in enumerate((sw_ref, st_ref)):
        for k in range(nf):
            loads[2 + i, k] = pltpu.make_async_copy(
                ref.at[pl.ds(k * cw, cw), :], w2.at[i, k], wsem.at[2 + i, k]
            )
    for pair in (0, 2):
        for k in range(nf):
            loads[pair, k].start()
            loads[pair + 1, k].start()

    sent = []

    def send(src, dst, ssem, rsem, device):
        copy = pltpu.make_async_remote_copy(
            src_ref=src, dst_ref=dst, send_sem=ssem, recv_sem=rsem,
            device_id=device, device_id_type=pl.DeviceIdType.MESH,
        )
        copy.start()
        sent.append(copy)
        return copy

    barrier = pltpu.get_barrier_semaphore()
    everyone = [mate] + across + peers
    for device in everyone:
        pl.semaphore_signal(
            barrier, inc=1, device_id=device, device_id_type=pl.DeviceIdType.MESH
        )
    pl.semaphore_wait(barrier, len(everyone))

    arrivals = [
        send(tok_ref, tokg.at[me], tok_s.at[o], tok_r.at[o], device)
        for o, device in enumerate(peers)
    ]
    tokg[me] = tok_ref[...]
    for copy in arrivals:
        copy.wait_recv()
    tok2d[...] = tokg[...].astype(F32).reshape(total, dl).astype(BF16)
    tok_out[...] = tok2d[...]

    cols = [pl.ds(k * cw, cw) for k in range(nf)]
    to_mate, to_chips, halves = {}, {}, {}

    def first(k):
        for i in range(2):
            loads[i, k].wait()
            hbuf[i, :, cols[k]] = jnp.dot(tok2d[...], w1[i, k], preferred_element_type=F32)
            psend[k, i] = hbuf[i, other, cols[k]]
        to_mate[k] = send(psend.at[k], precv.at[k], ps.at[k], pr.at[k], mate)

    def chip_sum(k):
        to_mate[k].wait_recv()
        for i in range(2):
            both = hbuf[i, mine, cols[k]] + precv[k, i]
            hbuf[i, mine, cols[k]] = both
            xsend[k, i] = both.astype(BF16)
        to_chips[k] = [
            send(xsend.at[k], xrecv.at[o, k], xs.at[o, k], xr.at[o, k], device)
            for o, device in enumerate(across)
        ]

    def activate(k):
        hidden, hidden_tan = hbuf[0, mine, cols[k]], hbuf[1, mine, cols[k]]
        for o, copy in enumerate(to_chips[k]):
            copy.wait_recv()
            hidden = hidden + xrecv[o, k, 0].astype(F32)
            hidden_tan = hidden_tan + xrecv[o, k, 1].astype(F32)
        active, active_tan, slope = gelu_parts(hidden, hidden_tan)
        acts[k, 0, mine, :] = active_tan.astype(BF16)
        acts[k, 1, mine, :] = active.astype(BF16)
        slopes[:, cols[k]] = slope
        part = acts.at[k, :, mine, :]
        halves[k] = send(part, part, as_.at[k], ar.at[k], mate)

    scatter, gather = {}, {}

    def second(k):
        halves[k].wait_recv()
        for i in range(2):
            loads[2 + i, k].wait()
        for n in range(no):
            part = pl.ds(n * dn, dn)
            term = jnp.dot(acts[k, 0], w2[0, k, :, part], preferred_element_type=F32)
            term += jnp.dot(acts[k, 1], w2[1, k, :, part], preferred_element_type=F32)
            if k > 0:
                term += acc[n]
            acc[n] = term
            if k == nf - 1:
                rsend[n] = term.reshape(group, tl, dn).astype(BF16)
                scatter[n] = [
                    send(rsend.at[n, r], rrecv.at[n, o], rs.at[n, o], rr.at[n, o], device)
                    for o, (r, device) in enumerate(zip(ranks, peers))
                ]

    for t in range(nf + 6):
        for lag, stage in ((0, first), (2, chip_sum), (4, activate), (6, second)):
            if 0 <= t - lag < nf:
                stage(t - lag)

    for n in range(no):
        value = acc[n, pl.ds(pl.multiple_of(me * tl, tl), tl), :]
        for o, copy in enumerate(scatter[n]):
            copy.wait_recv()
            value += rrecv[n, o].astype(F32)
        outg[n, me] = value.astype(BF16)
        gather[n] = [
            send(outg.at[n, me], outg.at[n, me], gs.at[n, o], gr.at[n, o], device)
            for o, device in enumerate(peers)
        ]

    to_mate, to_chips, halves = {}, {}, {}

    def back_chip_sum(k):
        to_mate[k].wait_recv()
        both = hbuf[0, mine, cols[k]] + brecv[k]
        hbuf[0, mine, cols[k]] = both
        bxsend[k] = both.astype(BF16)
        to_chips[k] = [
            send(bxsend.at[k], bxrecv.at[o, k], bxs.at[o, k], bxr.at[o, k], device)
            for o, device in enumerate(across)
        ]

    def back_finish(k):
        value = hbuf[0, mine, cols[k]]
        for o, copy in enumerate(to_chips[k]):
            copy.wait_recv()
            value += bxrecv[o, k].astype(F32)
        back[k, mine, :] = (value * slopes[:, cols[k]]).astype(BF16)
        part = back.at[k, mine, :]
        halves[k] = send(part, part, bas.at[k], bar_.at[k], mate)

    for n in range(no):
        for copy in gather[n]:
            copy.wait_recv()
        part = pl.ds(n * dn, dn)
        tan_out[:, part] = outg[n].astype(F32).reshape(total, dn).astype(BF16)
        for k in range(nf):
            term = lax.dot_general(
                tan_out[:, part], w2[0, k, :, part], (((1,), (1,)), ((), ())),
                preferred_element_type=F32,
            )
            if n > 0:
                term += hbuf[0, :, cols[k]]
            hbuf[0, :, cols[k]] = term
            if n == no - 1:
                bsend[k] = hbuf[0, other, cols[k]]
                to_mate[k] = send(bsend.at[k], brecv.at[k], bps.at[k], bpr.at[k], mate)
                if k >= 2:
                    back_chip_sum(k - 2)
                if k >= 5:
                    back_finish(k - 5)
    for k in range(max(0, nf - 2), nf):
        back_chip_sum(k)
    for k in range(max(0, nf - 5), nf):
        back_finish(k)
    for k in range(nf):
        act_out[k] = acts[k, 1]
    for k in range(nf):
        halves[k].wait_recv()
        back_out[k] = back[k]
    for copy in sent:
        copy.wait_send()


def grads_kernel(factor, tok_ref, act_ref, tan_ref, back_ref, first_ref, second_ref):
    lhs_rows = (((0,), (0,)), ((), ()))
    second_ref[...] = (
        lax.dot_general(act_ref[0], tan_ref[...], lhs_rows, preferred_element_type=F32) * factor
    )
    first_ref[...] = (
        lax.dot_general(tok_ref[...], back_ref[0], lhs_rows, preferred_element_type=F32) * factor
    )


def on_device(axes, tokens, first_weight, first_tangent, second_weight, second_tangent):
    tl, dl = tokens.shape
    fl = first_weight.shape[1]
    ncol, ndepth, chips = axes["col"], axes["depth"], axes["row"] // CORES
    group = ncol * ndepth
    total, half = group * tl, group * tl // CORES
    nf, no = pieces(fl, 6), pieces(dl, 3)
    cw, dn = fl // nf, dl // no
    far = max(chips - 1, 1)
    dma = pltpu.SemaphoreType.DMA
    whole = pl.BlockSpec(memory_space=pltpu.VMEM)
    hbm = pl.BlockSpec(memory_space=pl.ANY)
    gathered, active, out_tan, back_hidden = pl.pallas_call(
        functools.partial(block_kernel, (chips, ncol, ndepth, nf, no)),
        name="block",
        out_shape=(
            jax.ShapeDtypeStruct((total, dl), BF16),
            jax.ShapeDtypeStruct((nf, total, cw), BF16),
            jax.ShapeDtypeStruct((total, dl), BF16),
            jax.ShapeDtypeStruct((nf, total, cw), BF16),
        ),
        in_specs=[whole, hbm, hbm, hbm, hbm],
        out_specs=(whole,) * 4,
        scratch_shapes=[
            pltpu.VMEM((2, nf, dl, cw), BF16),
            pltpu.VMEM((2, nf, cw, dl), BF16),
            pltpu.VMEM((group, tl, dl), BF16),
            pltpu.VMEM((total, dl), BF16),
            pltpu.VMEM((2, total, fl), F32),
            pltpu.VMEM((nf, 2, half, cw), F32),
            pltpu.VMEM((nf, 2, half, cw), F32),
            pltpu.VMEM((nf, 2, half, cw), BF16),
            pltpu.VMEM((far, nf, 2, half, cw), BF16),
            pltpu.VMEM((nf, 2, total, cw), BF16),
            pltpu.VMEM((half, fl), F32),
            pltpu.VMEM((no, total, dn), F32),
            pltpu.VMEM((no, group, tl, dn), BF16),
            pltpu.VMEM((no, group - 1, tl, dn), BF16),
            pltpu.VMEM((no, group, tl, dn), BF16),
            pltpu.VMEM((nf, half, cw), F32),
            pltpu.VMEM((nf, half, cw), F32),
            pltpu.VMEM((nf, half, cw), BF16),
            pltpu.VMEM((far, nf, half, cw), BF16),
            pltpu.VMEM((nf, total, cw), BF16),
            dma((4, nf)),
            dma((group - 1,)), dma((group - 1,)),
            dma((nf,)), dma((nf,)),
            dma((far, nf)), dma((far, nf)),
            dma((nf,)), dma((nf,)),
            dma((no, group - 1)), dma((no, group - 1)),
            dma((no, group - 1)), dma((no, group - 1)),
            dma((nf,)), dma((nf,)),
            dma((far, nf)), dma((far, nf)),
            dma((nf,)), dma((nf,)),
        ],
        compiler_params=pltpu.CompilerParams(
            collective_id=0, has_side_effects=True, vmem_limit_bytes=62 * 1024 * 1024
        ),
    )(tokens, first_weight, first_tangent, second_weight, second_tangent)

    return pl.pallas_call(
        functools.partial(grads_kernel, 1.0 / math.sqrt(total)),
        name="grads",
        grid=(nf,),
        out_shape=(
            jax.ShapeDtypeStruct((dl, fl), F32),
            jax.ShapeDtypeStruct((fl, dl), F32),
        ),
        in_specs=[
            pl.BlockSpec((total, dl), lambda k: (0, 0)),
            pl.BlockSpec((1, total, cw), lambda k: (k, 0, 0)),
            pl.BlockSpec((total, dl), lambda k: (0, 0)),
            pl.BlockSpec((1, total, cw), lambda k: (k, 0, 0)),
        ],
        out_specs=(
            pl.BlockSpec((dl, cw), lambda k: (0, k)),
            pl.BlockSpec((cw, dl), lambda k: (k, 0)),
        ),
    )(gathered, active, out_tan, back_hidden)


def solution(mesh):
    return jax.shard_map(
        functools.partial(on_device, dict(mesh.shape)),
        mesh=mesh,
        in_specs=(
            P(("col", "depth"), "row"),
            P("row", ("col", "depth")),
            P("row", ("col", "depth")),
            P(("col", "depth"), "row"),
            P(("col", "depth"), "row"),
        ),
        out_specs=(P("row", ("col", "depth")), P(("col", "depth"), "row")),
        check_vma=False,
    )
```
